256 devices in a mesh: ja: 16 (over z, core), ka: 16 (over x, y).
Axes of the slice: x: 4, y: 4, z: 8, core: 2. Of those that a mesh axis runs over, the one named last changes fastest.
Arguments:
- tensor: float32 [64, 1024, 1024], P('ka', 'ja'), may hold values from -6 to 6
- factor_one: float32 [1024, 256], replicated, may hold values from -0.1875 to 0.1875
- factor_two: bfloat16 [1024, 256], P('ja'), may hold values from -0.1875 to 0.1875
Outputs:
- gram_one: float32 [1024, 1024], P(('ja', 'ka'))
- gram_two: float32 [1024, 1024], P(('ja', 'ka'))
- reduced: float32 [64, 256, 256], P('ka', 'ja')
The draws below stay inside these ranges and needn't reach their ends.
All inputs are finite; a program needn't handle non-finite values.
Results may differ from the reference program's by a relative error of at most 0.0029.
Values may be sent and summed in bfloat16 or wider, within the bound.
A program may use at most 64 MiB of HBM per device.

```python
import math
import jax
import jax.numpy as jnp
from jax import lax

N1 = 1024
N2 = 1024
R1 = 256
R2 = 256
N3 = 64


def levels(rng, shape, shards, least, top_value):
    factor_of = 1.0
    for axis_at, shards_of in shards:
        heights = jax.random.uniform(jax.random.fold_in(jax.random.fold_in(rng, 6), axis_at), (shards_of,), jnp.float32, least / len(shards), top_value / len(shards))
        factor_of = factor_of * jnp.repeat(jnp.exp(heights), shape[axis_at] // shards_of).reshape((-1,) + (1,) * (len(shape) - 1 - axis_at))
    return factor_of


def scatter_about(stream_key, shape, width, limit, shards=(), dtype=jnp.bfloat16):
    drawn = jax.random.normal(stream_key, shape, jnp.float32) * width
    if len(shards) > 0:
        drawn = levels(stream_key, shape, shards, -0.22, 0.18) * drawn
    return jnp.clip(drawn, min=-limit, max=limit).astype(dtype)


def setup_inputs(seed: int = 0) -> dict:
    arg_keys = jax.random.split(jax.random.key(seed), 4)
    return {
        "tensor": scatter_about(arg_keys[0], (N3, N2, N1), 1.0, 6.0, ((0, 16), (1, 16)), jnp.float32),
        "factor_one": scatter_about(arg_keys[1], (N1, R1), N1 ** -0.5, 0.1875, (), jnp.float32),
        "factor_two": scatter_about(arg_keys[2], (N2, R2), N2 ** -0.5, 0.1875, ((0, 16),)),
    }


def reference(tensor, factor_one, factor_two):
    flat = tensor.reshape(N3 * N2, N1)
    gram_one = jnp.dot(flat.T, flat, precision=lax.Precision.HIGHEST, preferred_element_type=jnp.float32)
    gram_one = gram_one * (1.0 / math.sqrt(N2 * N3))
    core = jnp.dot(flat, factor_one, precision=lax.Precision.HIGHEST, preferred_element_type=jnp.float32)
    core = core.astype(jnp.bfloat16).reshape(N3, N2, R1).astype(jnp.float32)
    gram_two = jnp.einsum('kjr,klr->jl', core, core, precision=lax.Precision.HIGHEST)
    gram_two = gram_two * (1.0 / math.sqrt(N3 * R1))
    reduced = jnp.einsum('kjr,js->ksr', core, factor_two.astype(jnp.float32), precision=lax.Precision.HIGHEST)
    return (gram_one, gram_two, reduced)
```

```python
import math

import jax
import jax.numpy as jnp
from jax import lax
from jax.experimental import pallas as pl
from jax.experimental.pallas import tpu as pltpu
from jax.sharding import PartitionSpec as P

MESH = pl.DeviceIdType.MESH
F32 = jnp.float32
BF16 = jnp.bfloat16


def hi_lo(x):
    hi = x.astype(BF16)
    return hi, (x - hi.astype(F32)).astype(BF16)


def groups_of_four(parts):
    rows, width = parts[0].shape
    n = rows // 8
    first = lax.broadcasted_iota(jnp.int32, (n, 8, width), 1) < 4

    def pair(a, b):
        a, b = a.reshape(n, 8, width), b.reshape(n, 8, width)
        low = jnp.where(first, a, pltpu.roll(b, 4, axis=1))
        high = jnp.where(first, pltpu.roll(a, 4, axis=1), b)
        return low, high

    low_a, high_a = pair(parts[0], parts[1])
    low_b, high_b = pair(parts[2], parts[3])
    return jnp.concatenate([low_a, low_b], axis=1), jnp.concatenate([high_a, high_b], axis=1)


def kernel(
    norms, sizes, tensor, factor_one, factor_two, gram_one, gram_two, reduced,
    x_v, f1_v, f2_v, lhs, rhs, part, to_sib, from_sib, to_plane, from_plane, to_line, from_line,
    core, f2_out, f2_in, g2_out, g2_in,
    load_sem, up_send, up_recv, down_send, down_recv, sib_send, sib_recv, half_send, half_recv,
    plane_send, plane_recv, line_send, line_recv, f2_send, f2_recv, g2_send, g2_recv,
):
    n_ja, n_ka = sizes
    n_z = n_ja // 2
    ja, ka = lax.axis_index("ja"), lax.axis_index("ka")
    z, c = ja // 2, ja % 2
    sib = z * 2 + (1 - c)
    loads = [
        pltpu.make_async_copy(src, dst, load_sem.at[i])
        for i, (src, dst) in enumerate(((tensor, x_v), (factor_one, f1_v), (factor_two, f2_v)))
    ]
    for load in loads:
        load.start()

    barrier = pltpu.get_barrier_semaphore()

    def greet_ja(d, carry):
        pl.semaphore_signal(barrier, inc=1, device_id={"ja": (ja + d) % n_ja}, device_id_type=MESH)
        return carry

    def greet_ka(d, carry):
        pl.semaphore_signal(barrier, inc=1, device_id={"ka": (ka + d) % n_ka}, device_id_type=MESH)
        return carry

    lax.fori_loop(1, n_ja, greet_ja, 0)
    lax.fori_loop(1, n_ka, greet_ka, 0)

    for load in loads:
        load.wait()
    x = x_v[...].reshape(256, 1024)
    x_hi, x_lo = hi_lo(x)
    rhs[0:256] = x_hi
    rhs[256:512] = x_lo
    rhs[512:768] = x_hi
    for block in range(8):
        turned = x[:, block * 128 : (block + 1) * 128].T
        t_hi, t_lo = hi_lo(turned)
        for half in range(2):
            rows = slice(half * 64, (half + 1) * 64)
            lhs[half, block, :, 0:256] = t_hi[rows]
            lhs[half, block, :, 256:512] = t_hi[rows]
            lhs[half, block, :, 512:768] = t_lo[rows]
    f_hi, f_lo = hi_lo(f1_v[...])
    mine = jnp.dot(x_hi, f_hi, preferred_element_type=F32)
    mine += jnp.dot(x_hi, f_lo, preferred_element_type=F32)
    mine += jnp.dot(x_lo, f_hi, preferred_element_type=F32)
    own_row = pl.multiple_of(ja * 64, 64)
    core[:, pl.ds(own_row, 64), :] = mine.astype(BF16).reshape(4, 64, 256)
    f2_out[...] = f2_v[...].astype(F32).T.astype(BF16).reshape(n_ja, 16, 64)
    f2_in[pl.ds(ja, 1)] = f2_out[pl.ds(ja, 1)]

    pl.semaphore_wait(barrier, n_ja + n_ka - 2)

    def block_of(chunk, source_z, source_c):
        row = pl.multiple_of(source_z * 128 + source_c * 64, 64)
        return core.at[pl.ds(chunk * 2, 2), pl.ds(row, 64), :]

    def ring_copy(up, chunk, hop):
        source = (z - (hop - 1) + n_z) % n_z if up else (z + (hop - 1)) % n_z
        target = (z + 1) % n_z if up else (z - 1 + n_z) % n_z
        block = block_of(chunk, source, c)
        send, recv = (up_send, up_recv) if up else (down_send, down_recv)
        return pltpu.make_async_remote_copy(
            block, block, send.at[chunk, hop - 1], recv.at[chunk, hop - 1],
            device_id={"ja": target * 2 + c}, device_id_type=MESH,
        )

    def arrival(up, chunk, hop):
        source = (z - hop + n_z) % n_z if up else (z + hop) % n_z
        block = block_of(chunk, source, c)
        send, recv = (up_send, up_recv) if up else (down_send, down_recv)
        return pltpu.make_async_remote_copy(
            block, block, send.at[chunk, hop - 1], recv.at[chunk, hop - 1],
            device_id={"ja": sib}, device_id_type=MESH,
        )

    def sib_copy(chunk, source_z, slot, source_c):
        block = block_of(chunk, source_z, source_c)
        return pltpu.make_async_remote_copy(
            block, block, sib_send.at[chunk, slot], sib_recv.at[chunk, slot],
            device_id={"ja": sib}, device_id_type=MESH,
        )

    last_hop = {(True, 0): 4, (True, 1): 3, (False, 0): 3, (False, 1): 4}
    for chunk in range(2):
        for up in (True, False):
            ring_copy(up, chunk, 1).start()
    for chunk in range(2):
        sib_copy(chunk, z, 0, c).start()

    def f2_copy(d):
        to = (ja + d) % n_ja
        return pltpu.make_async_remote_copy(
            f2_out.at[to], f2_in.at[ja], f2_send.at[to], f2_recv.at[ja],
            device_id={"ja": to}, device_id_type=MESH,
        )

    def f2_arrival(d):
        source = (ja + d) % n_ja
        return pltpu.make_async_remote_copy(
            f2_out.at[source], f2_in.at[source], f2_send.at[source], f2_recv.at[source],
            device_id={"ja": source}, device_id_type=MESH,
        )

    def start_f2(d, carry):
        f2_copy(d).start()
        return carry

    lax.fori_loop(1, n_ja, start_f2, 0)

    def product(half):
        left = lhs[half].reshape(512, 768)
        for block in range(4):
            columns = slice(block * 256, (block + 1) * 256)
            part[:, :, columns] = jnp.dot(left, rhs[:, columns], preferred_element_type=F32).reshape(8, 64, 256)

    pair = ka // 2

    def rows_of(m):
        at = pl.ds(pl.multiple_of(m * 8, 8), 8)
        low_a, high_a = groups_of_four([part[i, at, :] for i in range(4)])
        low_b, high_b = groups_of_four([part[4 + i, at, :] for i in range(4)])
        return (
            jnp.concatenate([low_a[0], low_b[0]], axis=0),
            jnp.concatenate([high_a[0], high_b[0]], axis=0),
        )

    def half_copy(m):
        return pltpu.make_async_remote_copy(
            to_sib.at[m], from_sib.at[m], half_send.at[m], half_recv.at[m],
            device_id={"ja": sib}, device_id_type=MESH,
        )

    product(1 - c)

    def give(dm, carry):
        m = (pair + dm) % 8
        low, high = rows_of(m)
        to_sib[m, 0] = low.astype(BF16)
        to_sib[m, 1] = high.astype(BF16)
        half_copy(m).start()
        return carry

    lax.fori_loop(1, 9, give, 0)
    product(c)

    def plane_copy(to):
        return pltpu.make_async_remote_copy(
            to_plane.at[to // 2, to % 2], from_plane.at[ka], plane_send.at[to], plane_recv.at[ka],
            device_id={"ka": to}, device_id_type=MESH,
        )

    def plane_arrival(source):
        return pltpu.make_async_remote_copy(
            to_plane.at[source // 2, source % 2], from_plane.at[source], plane_send.at[source],
            plane_recv.at[source], device_id={"ka": source}, device_id_type=MESH,
        )

    def combine(m):
        half_copy(m).wait_recv()
        low, high = rows_of(m)
        to_plane[m, 0] = (low + from_sib[m, 0].astype(F32)).astype(BF16)
        to_plane[m, 1] = (high + from_sib[m, 1].astype(F32)).astype(BF16)

    def give_plane(dm, carry):
        m = (pair + dm) % 8
        combine(m)
        plane_copy(m * 2).start()
        plane_copy(m * 2 + 1).start()
        return carry

    lax.fori_loop(1, 8, give_plane, 0)
    combine(pair)
    plane_copy(pair * 2 + 1 - ka % 2).start()

    for hop in range(1, 5):
        for chunk in range(2):
            for up in (True, False):
                if hop > last_hop[up, chunk]:
                    continue
                arrival(up, chunk, hop).wait_recv()
                if hop < last_hop[up, chunk]:
                    ring_copy(up, chunk, hop + 1).start()
                source = (z - hop + n_z) % n_z if up else (z + hop) % n_z
                sib_copy(chunk, source, hop if up else n_z - hop, c).start()
    for slot in range(8):
        for chunk in range(2):
            sib_copy(chunk, (z - slot + n_z) % n_z, slot, 1 - c).wait_recv()

    own = core[:, pl.ds(own_row, 64), :]
    sums = []
    for block in range(4):
        columns = slice(block * 256, (block + 1) * 256)
        total = jnp.zeros((64, 256), F32)
        for k in range(4):
            total += lax.dot_general(
                own[k], core[k, columns, :], (((1,), (1,)), ((), ())), preferred_element_type=F32
            )
        sums.append(total)
    low, high = groups_of_four(sums)
    g2_out[:, 0] = low.astype(BF16)
    g2_out[:, 1] = high.astype(BF16)

    def g2_copy(to):
        return pltpu.make_async_remote_copy(
            g2_out.at[to // 2, to % 2], g2_in.at[ka], g2_send.at[to], g2_recv.at[ka],
            device_id={"ka": to}, device_id_type=MESH,
        )

    def g2_arrival(source):
        return pltpu.make_async_remote_copy(
            g2_out.at[source // 2, source % 2], g2_in.at[source], g2_send.at[source], g2_recv.at[source],
            device_id={"ka": source}, device_id_type=MESH,
        )

    def start_g2(d, carry):
        g2_copy((ka + d) % n_ka).start()
        return carry

    lax.fori_loop(1, n_ka, start_g2, 0)

    def end_f2(d, carry):
        f2_arrival(d).wait_recv()
        return carry

    lax.fori_loop(1, n_ja, end_f2, 0)
    f2 = jnp.concatenate([f2_in[i].astype(F32) for i in range(n_ja)], axis=1).astype(BF16)
    for k in range(4):
        reduced[k] = jnp.dot(f2, core[k], preferred_element_type=F32)

    def add_plane(d, total):
        source = (ka + d) % n_ka
        plane_arrival(source).wait_recv()
        return total + from_plane[source].astype(F32)

    total = lax.fori_loop(1, n_ka, add_plane, to_plane[pair, ka % 2].astype(F32))
    low, high = groups_of_four([total[:, i * 256 : (i + 1) * 256] for i in range(4)])
    to_line[:, 0] = low.astype(BF16)
    to_line[:, 1] = high.astype(BF16)

    def line_copy(to):
        return pltpu.make_async_remote_copy(
            to_line.at[to // 2, to % 2], from_line.at[z], line_send.at[to], line_recv.at[z],
            device_id={"ja": to * 2 + c}, device_id_type=MESH,
        )

    def line_arrival(source):
        return pltpu.make_async_remote_copy(
            to_line.at[source // 2, source % 2], from_line.at[source], line_send.at[source],
            line_recv.at[source], device_id={"ja": source * 2 + c}, device_id_type=MESH,
        )

    def start_line(d, carry):
        line_copy((z + d) % n_z).start()
        return carry

    lax.fori_loop(1, n_z, start_line, 0)

    def add_g2(d, total):
        source = (ka + d) % n_ka
        g2_arrival(source).wait_recv()
        return total + g2_in[source].astype(F32)

    total = lax.fori_loop(1, n_ka, add_g2, g2_out[pair, ka % 2].astype(F32)) * norms[1]
    for i in range(4):
        gram_two[:, i * 256 : (i + 1) * 256] = total[i * 4 : (i + 1) * 4]

    def add_line(d, total):
        source = (z + d) % n_z
        line_arrival(source).wait_recv()
        return total + from_line[source].astype(F32)

    total = lax.fori_loop(1, n_z, add_line, to_line[z // 2, z % 2].astype(F32)) * norms[0]
    for i in range(4):
        gram_one[:, i * 256 : (i + 1) * 256] = total[i * 4 : (i + 1) * 4]

    for chunk in range(2):
        for up in (True, False):
            for hop in range(1, last_hop[up, chunk] + 1):
                ring_copy(up, chunk, hop).wait_send()
        for slot in range(8):
            sib_copy(chunk, (z - slot + n_z) % n_z, slot, c).wait_send()

    def end_ja(d, carry):
        f2_copy(d).wait_send()
        return carry

    def end_ka(d, carry):
        to = (ka + d) % n_ka
        plane_copy(to).wait_send()
        g2_copy(to).wait_send()
        return carry

    def end_z(d, carry):
        line_copy((z + d) % n_z).wait_send()
        return carry

    def end_half(m, carry):
        half_copy(m).wait_send()
        return carry

    lax.fori_loop(1, n_ja, end_ja, 0)
    lax.fori_loop(1, n_ka, end_ka, 0)
    lax.fori_loop(1, n_z, end_z, 0)
    lax.fori_loop(0, 8, end_half, 0)


def solution(mesh):
    n_ja, n_ka = mesh.shape["ja"], mesh.shape["ka"]

    def shards(tensor, factor_one, factor_two):
        slices, owned, width = tensor.shape
        norm_one = 1.0 / math.sqrt(owned * n_ja * slices * n_ka)
        norm_two = 1.0 / math.sqrt(slices * n_ka * factor_one.shape[1])
        dma = pltpu.SemaphoreType.DMA

        def body(*refs):
            kernel((norm_one, norm_two), (n_ja, n_ka), *refs)

        return pl.pallas_call(
            body,
            out_shape=(
                jax.ShapeDtypeStruct((4, 1024), F32),
                jax.ShapeDtypeStruct((4, 1024), F32),
                jax.ShapeDtypeStruct((4, 16, 256), F32),
            ),
            in_specs=[pl.BlockSpec(memory_space=pl.ANY)] * 3,
            out_specs=[pl.BlockSpec(memory_space=pltpu.VMEM)] * 3,
            scratch_shapes=[
                pltpu.VMEM((4, 64, 1024), F32),
                pltpu.VMEM((1024, 256), F32),
                pltpu.VMEM((64, 256), BF16),
                pltpu.VMEM((2, 8, 64, 768), BF16),
                pltpu.VMEM((768, 1024), BF16),
                pltpu.VMEM((8, 64, 1024), F32),
                pltpu.VMEM((8, 2, 32, 1024), BF16),
                pltpu.VMEM((8, 2, 32, 1024), BF16),
                pltpu.VMEM((8, 2, 32, 1024), BF16),
                pltpu.VMEM((16, 32, 1024), BF16),
                pltpu.VMEM((4, 2, 16, 256), BF16),
                pltpu.VMEM((8, 16, 256), BF16),
                pltpu.VMEM((4, 1024, 256), BF16),
                pltpu.VMEM((16, 16, 64), BF16),
                pltpu.VMEM((16, 16, 64), BF16),
                pltpu.VMEM((8, 2, 16, 256), BF16),
                pltpu.VMEM((16, 16, 256), BF16),
                dma((3,)),
                dma((2, 4)), dma((2, 4)), dma((2, 4)), dma((2, 4)),
                dma((2, 8)), dma((2, 8)),
                dma((8,)), dma((8,)),
                dma((16,)), dma((16,)),
                dma((8,)), dma((8,)),
                dma((16,)), dma((16,)),
                dma((16,)), dma((16,)),
            ],
            compiler_params=pltpu.CompilerParams(
                collective_id=0, has_side_effects=True, vmem_limit_bytes=48 * 1024 * 1024
            ),
        )(tensor, factor_one, factor_two)

    return jax.shard_map(
        shards,
        mesh=mesh,
        in_specs=(P("ka", "ja", None), P(), P("ja", None)),
        out_specs=(P(("ja", "ka"), None), P(("ja", "ka"), None), P("ka", "ja", None)),
        check_vma=False,
    )
```

```python
import math

import jax
import jax.numpy as jnp
from jax import lax
from jax.experimental import pallas as pl
from jax.experimental.pallas import tpu as pltpu
from jax.sharding import PartitionSpec as P

MESH = pl.DeviceIdType.MESH
F32 = jnp.float32
BF16 = jnp.bfloat16


def hi_lo(x):
    hi = x.astype(BF16)
    return hi, (x - hi.astype(F32)).astype(BF16)


def groups_of_four(parts):
    rows, width = parts[0].shape
    n = rows // 8
    first = lax.broadcasted_iota(jnp.int32, (n, 8, width), 1) < 4

    def pair(a, b):
        a, b = a.reshape(n, 8, width), b.reshape(n, 8, width)
        low = jnp.where(first, a, pltpu.roll(b, 4, axis=1))
        high = jnp.where(first, pltpu.roll(a, 4, axis=1), b)
        return low, high

    low_a, high_a = pair(parts[0], parts[1])
    low_b, high_b = pair(parts[2], parts[3])
    return jnp.concatenate([low_a, low_b], axis=1), jnp.concatenate([high_a, high_b], axis=1)


def kernel(
    norms, sizes, tensor, factor_one, factor_two, gram_one, gram_two, reduced,
    x_v, f1_v, f2_v, lhs, rhs, part, to_sib, from_sib, to_plane, far, near, to_cross, far_cross, near_cross,
    to_line, from_line, core, f2_out, f2_in, g2_out, g2_in, known,
    load_sem, up_send, up_recv, down_send, down_recv, sib_send, sib_recv, half_send, half_recv,
    plane_send, plane_recv, cross_send, cross_recv, line_send, line_recv, f2_send, f2_recv, g2_send, g2_recv,
):
    n_ja, n_ka = sizes
    n_z = n_ja // 2
    ja, ka = lax.axis_index("ja"), lax.axis_index("ka")
    z, c = ja // 2, ja % 2
    sib = z * 2 + (1 - c)
    loads = [
        pltpu.make_async_copy(src, dst, load_sem.at[i])
        for i, (src, dst) in enumerate(((tensor, x_v), (factor_one, f1_v), (factor_two, f2_v)))
    ]
    for load in loads:
        load.start()

    barrier = pltpu.get_barrier_semaphore()

    x, y = ka // 4, ka % 4
    z_next = [((z + step) % n_z) * 2 + c for step in (1, n_z - 1)]
    x_next = [((x + step) % 4) * 4 + y for step in (1, 3)]
    y_next = [x * 4 + (y + step) % 4 for step in (1, 3)]

    def tell(semaphore, axis, peers):
        for peer in peers:
            pl.semaphore_signal(semaphore, inc=1, device_id={axis: peer}, device_id_type=MESH)

    tell(barrier, "ja", [sib] + z_next)
    tell(barrier, "ka", x_next + y_next)

    def learn(step):
        if step > 0:
            pl.semaphore_wait(known.at[0, step - 1], 2)
            pl.semaphore_wait(known.at[1, step - 1], 2)
        if step < 3:
            tell(known.at[0, step], "ka", x_next if step == 0 else y_next)
            tell(known.at[1, step], "ja", z_next)
        else:
            tell(known.at[1, 3], "ja", [sib])

    for load in loads:
        load.wait()
    x_hi, x_lo = hi_lo(x_v[...].reshape(256, 1024))
    f_hi, f_lo = hi_lo(f1_v[...])
    mine = jnp.dot(x_hi, f_hi, preferred_element_type=F32)
    mine += jnp.dot(x_hi, f_lo, preferred_element_type=F32)
    mine += jnp.dot(x_lo, f_hi, preferred_element_type=F32)
    own_row = pl.multiple_of(ja * 64, 64)
    core[:, pl.ds(own_row, 64), :] = mine.astype(BF16).reshape(4, 64, 256)
    f2_out[...] = f2_v[...].astype(F32).T.astype(BF16).reshape(n_ja, 16, 64)
    f2_in[pl.ds(ja, 1)] = f2_out[pl.ds(ja, 1)]

    pl.semaphore_wait(barrier, 7)

    def block_of(chunk, source_z, source_c):
        row = pl.multiple_of(source_z * 128 + source_c * 64, 64)
        return core.at[chunk, pl.ds(row, 64), :]

    def ring_copy(up, chunk, hop):
        source = (z - (hop - 1) + n_z) % n_z if up else (z + (hop - 1)) % n_z
        target = (z + 1) % n_z if up else (z - 1 + n_z) % n_z
        block = block_of(chunk, source, c)
        send, recv = (up_send, up_recv) if up else (down_send, down_recv)
        return pltpu.make_async_remote_copy(
            block, block, send.at[chunk, hop - 1], recv.at[chunk, hop - 1],
            device_id={"ja": target * 2 + c}, device_id_type=MESH,
        )

    def arrival(up, chunk, hop):
        source = (z - hop + n_z) % n_z if up else (z + hop) % n_z
        block = block_of(chunk, source, c)
        send, recv = (up_send, up_recv) if up else (down_send, down_recv)
        return pltpu.make_async_remote_copy(
            block, block, send.at[chunk, hop - 1], recv.at[chunk, hop - 1],
            device_id={"ja": sib}, device_id_type=MESH,
        )

    def sib_copy(chunk, source_z, slot, source_c):
        block = block_of(chunk, source_z, source_c)
        return pltpu.make_async_remote_copy(
            block, block, sib_send.at[chunk, slot], sib_recv.at[chunk, slot],
            device_id={"ja": sib}, device_id_type=MESH,
        )

    def last_hop(up, chunk):
        return 4 if up == (chunk < 2) else 3

    order = [(up, chunk) for pair in zip((0, 1, 2, 3), (2, 3, 0, 1)) for up, chunk in zip((True, False), pair)]
    for up, chunk in order:
        ring_copy(up, chunk, 1).start()
    for chunk in range(4):
        sib_copy(chunk, z, 0, c).start()
    learn(0)

    def pass_on(hop):
        for up, chunk in order:
            if hop > last_hop(up, chunk):
                continue
            arrival(up, chunk, hop).wait_recv()
            if hop < last_hop(up, chunk):
                ring_copy(up, chunk, hop + 1).start()
            source = (z - hop + n_z) % n_z if up else (z + hop) % n_z
            sib_copy(chunk, source, hop if up else n_z - hop, c).start()

    rhs[0:256] = x_hi
    rhs[256:512] = x_lo
    rhs[512:768] = x_hi
    for block in range(8):
        turned = x_v[:, :, block * 128 : (block + 1) * 128].reshape(256, 128).T
        t_hi, t_lo = hi_lo(turned)
        for half in range(2):
            rows = slice(half * 64, (half + 1) * 64)
            lhs[half, block, :, 0:256] = t_hi[rows]
            lhs[half, block, :, 256:512] = t_hi[rows]
            lhs[half, block, :, 512:768] = t_lo[rows]

    def f2_copy(d):
        to = (ja + d) % n_ja
        return pltpu.make_async_remote_copy(
            f2_out.at[to], f2_in.at[ja], f2_send.at[to], f2_recv.at[ja],
            device_id={"ja": to}, device_id_type=MESH,
        )

    def f2_arrival(d):
        source = (ja + d) % n_ja
        return pltpu.make_async_remote_copy(
            f2_out.at[source], f2_in.at[source], f2_send.at[source], f2_recv.at[source],
            device_id={"ja": source}, device_id_type=MESH,
        )

    def start_f2(d, carry):
        f2_copy(d).start()
        return carry

    def product(half):
        left = lhs[half].reshape(512, 768)
        for block in range(4):
            columns = slice(block * 256, (block + 1) * 256)
            part[:, :, columns] = jnp.dot(left, rhs[:, columns], preferred_element_type=F32).reshape(8, 64, 256)

    def rows_of(m):
        at = pl.ds(pl.multiple_of(m * 8, 8), 8)
        low_a, high_a = groups_of_four([part[i, at, :] for i in range(4)])
        low_b, high_b = groups_of_four([part[4 + i, at, :] for i in range(4)])
        return (
            jnp.concatenate([low_a[0], low_b[0]], axis=0),
            jnp.concatenate([high_a[0], high_b[0]], axis=0),
        )

    def half_copy(m):
        return pltpu.make_async_remote_copy(
            to_sib.at[m], from_sib.at[m], half_send.at[m], half_recv.at[m],
            device_id={"ja": sib}, device_id_type=MESH,
        )

    product(1 - c)

    def give(row):
        def body(h, carry):
            m = row * 2 + h
            low, high = rows_of(m)
            to_sib[m, 0] = low.astype(BF16)
            to_sib[m, 1] = high.astype(BF16)
            half_copy(m).start()
            return carry

        lax.fori_loop(0, 2, body, 0)

    for step in (2, 1, 3, 0):
        give((x + step) % 4)
    learn(1)
    pass_on(1)
    product(c)
    learn(2)

    def half_of(left, half):
        return slice(left + half * 256, left + (half + 1) * 256)

    def slab(axis, at, lanes):
        return (pl.ds(at, 1), slice(None), slice(None), lanes) if axis == 0 else (slice(None), pl.ds(at, 1), slice(None), lanes)

    def plane_copy(axis, way, kind):
        place = x if axis == 0 else y
        to = (place + (1, 3)[way]) % 4
        peer = (x_next, y_next)[axis][way]
        at = (place + 2) % 4 if kind == 0 else to
        half = 1 - way if kind == 1 else way
        lanes = half_of(axis * 512, half)
        source = to_plane.at[at, :, :, lanes] if axis == 0 else to_plane.at[:, at, :, lanes]
        target = far.at[axis, way] if kind == 0 else near.at[axis, way, :, :, half_of(0, half)]
        return pltpu.make_async_remote_copy(
            source, target, plane_send.at[axis, way, kind], plane_recv.at[axis, way, kind],
            device_id={"ka": peer}, device_id_type=MESH,
        )

    def cross_copy(axis, way, kind):
        place = y if axis == 0 else x
        to = (place + (1, 3)[way]) % 4
        peer = (y_next, x_next)[axis][way]
        at = (place + 2) % 4 if kind == 0 else to
        half = 1 - way if kind == 1 else way
        target = far_cross.at[axis, way] if kind == 0 else near_cross.at[axis, way, :, half_of(0, half)]
        return pltpu.make_async_remote_copy(
            to_cross.at[axis, at, :, half_of(0, half)], target,
            cross_send.at[axis, way, kind], cross_recv.at[axis, way, kind],
            device_id={"ka": peer}, device_id_type=MESH,
        )

    def combine(row):
        def body(h, carry):
            m = row * 2 + h
            half_copy(m).wait_recv()
            low, high = rows_of(m)
            to_plane[row, h * 2] = (low + from_sib[m, 0].astype(F32)).astype(BF16)
            to_plane[row, h * 2 + 1] = (high + from_sib[m, 1].astype(F32)).astype(BF16)
            return carry

        lax.fori_loop(0, 2, body, 0)

    combine((x + 2) % 4)
    for way in range(2):
        plane_copy(0, way, 0).start()
    combine((x + 1) % 4)
    plane_copy(0, 0, 1).start()
    combine((x + 3) % 4)
    plane_copy(0, 1, 1).start()
    combine(x)
    for kind in range(2):
        for way in range(2):
            plane_copy(1, way, kind).start()
    learn(3)
    pass_on(2)

    pl.semaphore_wait(known.at[1, 3], 1)
    lax.fori_loop(1, n_ja, start_f2, 0)

    for axis in range(2):
        place = x if axis == 0 else y
        for way in range(2):
            plane_copy(axis, way, 0).wait_recv()
            where = slab(axis, (place + (1, 3)[way]) % 4, half_of(axis * 512, way))
            mine = to_plane[where]
            to_plane[where] = (mine.astype(F32) + far[axis, way].reshape(mine.shape).astype(F32)).astype(BF16)
            plane_copy(axis, way, 2).start()
    pass_on(3)
    for axis in range(2):
        for way in range(2):
            for kind in (1, 2):
                plane_copy(axis, way, kind).wait_recv()
        mine = to_plane[slab(axis, x if axis == 0 else y, slice(axis * 512, axis * 512 + 512))].reshape(4, 32, 512)
        to_cross[axis] = (mine.astype(F32) + near[axis, 0].astype(F32) + near[axis, 1].astype(F32)).astype(BF16)
        for kind in range(2):
            for way in range(2):
                cross_copy(axis, way, kind).start()
    pass_on(4)

    for slot in range(8):
        for chunk in range(4):
            sib_copy(chunk, (z - slot + n_z) % n_z, slot, 1 - c).wait_recv()

    own = core[:, pl.ds(own_row, 64), :]
    sums = []
    for block in range(4):
        columns = slice(block * 256, (block + 1) * 256)
        total = jnp.zeros((64, 256), F32)
        for k in range(4):
            total += lax.dot_general(
                own[k], core[k, columns, :], (((1,), (1,)), ((), ())), preferred_element_type=F32
            )
        sums.append(total)
    low, high = groups_of_four(sums)
    g2_out[:, 0] = low.astype(BF16)
    g2_out[:, 1] = high.astype(BF16)

    def g2_copy(to):
        return pltpu.make_async_remote_copy(
            g2_out.at[to // 2, to % 2], g2_in.at[ka], g2_send.at[to], g2_recv.at[ka],
            device_id={"ka": to}, device_id_type=MESH,
        )

    def g2_arrival(source):
        return pltpu.make_async_remote_copy(
            g2_out.at[source // 2, source % 2], g2_in.at[source], g2_send.at[source], g2_recv.at[source],
            device_id={"ka": source}, device_id_type=MESH,
        )

    def start_g2(d, carry):
        g2_copy((ka + d) % n_ka).start()
        return carry

    lax.fori_loop(1, n_ka, start_g2, 0)

    for axis in range(2):
        place = y if axis == 0 else x
        for way in range(2):
            cross_copy(axis, way, 0).wait_recv()
            where = (axis, (place + (1, 3)[way]) % 4, slice(None), half_of(0, way))
            to_cross[where] = (to_cross[where].astype(F32) + far_cross[axis, way].astype(F32)).astype(BF16)
            cross_copy(axis, way, 2).start()

    def end_f2(d, carry):
        f2_arrival(d).wait_recv()
        return carry

    lax.fori_loop(1, n_ja, end_f2, 0)
    f2 = jnp.concatenate([f2_in[i].astype(F32) for i in range(n_ja)], axis=1).astype(BF16)
    for k in range(4):
        reduced[k] = jnp.dot(f2, core[k], preferred_element_type=F32)

    sides = []
    for axis in range(2):
        for way in range(2):
            for kind in (1, 2):
                cross_copy(axis, way, kind).wait_recv()
        mine = to_cross[axis, y if axis == 0 else x]
        sides.append(mine.astype(F32) + near_cross[axis, 0].astype(F32) + near_cross[axis, 1].astype(F32))
    total = jnp.concatenate(sides, axis=1)
    low, high = groups_of_four([total[:, i * 256 : (i + 1) * 256] for i in range(4)])
    to_line[:, 0] = low.astype(BF16)
    to_line[:, 1] = high.astype(BF16)

    def line_copy(to):
        return pltpu.make_async_remote_copy(
            to_line.at[to // 2, to % 2], from_line.at[z], line_send.at[to], line_recv.at[z],
            device_id={"ja": to * 2 + c}, device_id_type=MESH,
        )

    def line_arrival(source):
        return pltpu.make_async_remote_copy(
            to_line.at[source // 2, source % 2], from_line.at[source], line_send.at[source],
            line_recv.at[source], device_id={"ja": source * 2 + c}, device_id_type=MESH,
        )

    def start_line(d, carry):
        line_copy((z + d) % n_z).start()
        return carry

    lax.fori_loop(1, n_z, start_line, 0)

    def add_g2(d, total):
        source = (ka + d) % n_ka
        g2_arrival(source).wait_recv()
        return total + g2_in[source].astype(F32)

    total = lax.fori_loop(1, n_ka, add_g2, g2_out[ka // 2, ka % 2].astype(F32)) * norms[1]
    for i in range(4):
        gram_two[:, i * 256 : (i + 1) * 256] = total[i * 4 : (i + 1) * 4]

    def add_line(d, total):
        source = (z + d) % n_z
        line_arrival(source).wait_recv()
        return total + from_line[source].astype(F32)

    total = lax.fori_loop(1, n_z, add_line, to_line[z // 2, z % 2].astype(F32)) * norms[0]
    for i in range(4):
        gram_one[:, i * 256 : (i + 1) * 256] = total[i * 4 : (i + 1) * 4]

    for chunk in range(4):
        for up in (True, False):
            for hop in range(1, last_hop(up, chunk) + 1):
                ring_copy(up, chunk, hop).wait_send()
        for slot in range(8):
            sib_copy(chunk, (z - slot + n_z) % n_z, slot, c).wait_send()
    for axis in range(2):
        for way in range(2):
            for kind in range(3):
                plane_copy(axis, way, kind).wait_send()
                cross_copy(axis, way, kind).wait_send()

    def end_ja(d, carry):
        f2_copy(d).wait_send()
        return carry

    def end_ka(d, carry):
        g2_copy((ka + d) % n_ka).wait_send()
        return carry

    def end_z(d, carry):
        line_copy((z + d) % n_z).wait_send()
        return carry

    def end_half(m, carry):
        half_copy(m).wait_send()
        return carry

    lax.fori_loop(1, n_ja, end_ja, 0)
    lax.fori_loop(1, n_ka, end_ka, 0)
    lax.fori_loop(1, n_z, end_z, 0)
    lax.fori_loop(0, 8, end_half, 0)


def solution(mesh):
    n_ja, n_ka = mesh.shape["ja"], mesh.shape["ka"]

    def shards(tensor, factor_one, factor_two):
        slices, owned, width = tensor.shape
        norm_one = 1.0 / math.sqrt(owned * n_ja * slices * n_ka)
        norm_two = 1.0 / math.sqrt(slices * n_ka * factor_one.shape[1])
        dma = pltpu.SemaphoreType.DMA

        def body(*refs):
            kernel((norm_one, norm_two), (n_ja, n_ka), *refs)

        return pl.pallas_call(
            body,
            out_shape=(
                jax.ShapeDtypeStruct((4, 1024), F32),
                jax.ShapeDtypeStruct((4, 1024), F32),
                jax.ShapeDtypeStruct((4, 16, 256), F32),
            ),
            in_specs=[pl.BlockSpec(memory_space=pl.ANY)] * 3,
            out_specs=[pl.BlockSpec(memory_space=pltpu.VMEM)] * 3,
            scratch_shapes=[
                pltpu.VMEM((4, 64, 1024), F32),
                pltpu.VMEM((1024, 256), F32),
                pltpu.VMEM((64, 256), BF16),
                pltpu.VMEM((2, 8, 64, 768), BF16),
                pltpu.VMEM((768, 1024), BF16),
                pltpu.VMEM((8, 64, 1024), F32),
                pltpu.VMEM((8, 2, 32, 1024), BF16),
                pltpu.VMEM((8, 2, 32, 1024), BF16),
                pltpu.VMEM((4, 4, 32, 1024), BF16),
                pltpu.VMEM((2, 2, 4, 32, 256), BF16),
                pltpu.VMEM((2, 2, 4, 32, 512), BF16),
                pltpu.VMEM((2, 4, 32, 512), BF16),
                pltpu.VMEM((2, 2, 32, 256), BF16),
                pltpu.VMEM((2, 2, 32, 512), BF16),
                pltpu.VMEM((4, 2, 16, 256), BF16),
                pltpu.VMEM((8, 16, 256), BF16),
                pltpu.VMEM((4, 1024, 256), BF16),
                pltpu.VMEM((16, 16, 64), BF16),
                pltpu.VMEM((16, 16, 64), BF16),
                pltpu.VMEM((8, 2, 16, 256), BF16),
                pltpu.VMEM((16, 16, 256), BF16),
                pltpu.SemaphoreType.REGULAR((2, 4)),
                dma((3,)),
                dma((4, 4)), dma((4, 4)), dma((4, 4)), dma((4, 4)),
                dma((4, 8)), dma((4, 8)),
                dma((8,)), dma((8,)),
                dma((2, 2, 3)), dma((2, 2, 3)),
                dma((2, 2, 3)), dma((2, 2, 3)),
                dma((8,)), dma((8,)),
                dma((16,)), dma((16,)),
                dma((16,)), dma((16,)),
            ],
            compiler_params=pltpu.CompilerParams(
                collective_id=0, has_side_effects=True, vmem_limit_bytes=48 * 1024 * 1024
            ),
        )(tensor, factor_one, factor_two)

    return jax.shard_map(
        shards,
        mesh=mesh,
        in_specs=(P("ka", "ja", None), P(), P("ja", None)),
        out_specs=(P(("ja", "ka"), None), P(("ja", "ka"), None), P("ka", "ja", None)),
        check_vma=False,
    )
```

```python
import math

import jax
import jax.numpy as jnp
from jax import lax
from jax.experimental import pallas as pl
from jax.experimental.pallas import tpu as pltpu
from jax.sharding import PartitionSpec as P

MESH = pl.DeviceIdType.MESH
F32 = jnp.float32
BF16 = jnp.bfloat16


def hi_lo(x):
    hi = x.astype(BF16)
    return hi, (x - hi.astype(F32)).astype(BF16)


def groups_of_four(parts):
    rows, width = parts[0].shape
    n = rows // 8
    first = lax.broadcasted_iota(jnp.int32, (n, 8, width), 1) < 4

    def pair(a, b):
        a, b = a.reshape(n, 8, width), b.reshape(n, 8, width)
        low = jnp.where(first, a, pltpu.roll(b, 4, axis=1))
        high = jnp.where(first, pltpu.roll(a, 4, axis=1), b)
        return low, high

    low_a, high_a = pair(parts[0], parts[1])
    low_b, high_b = pair(parts[2], parts[3])
    return jnp.concatenate([low_a, low_b], axis=1), jnp.concatenate([high_a, high_b], axis=1)


def kernel(
    norms, sizes, tensor, factor_one, factor_two, gram_one, gram_two, reduced,
    x_v, f1_v, f2_v, lhs, rhs, part, to_sib, from_sib, to_plane, far, near, to_cross, far_cross, near_cross,
    to_line, from_line, core, f2_out, f2_in, g2_out, g2_in,
    load_sem, up_send, up_recv, down_send, down_recv, sib_send, sib_recv, half_send, half_recv,
    plane_send, plane_recv, cross_send, cross_recv, line_send, line_recv, f2_send, f2_recv, g2_send, g2_recv,
):
    n_ja, n_ka = sizes
    n_z = n_ja // 2
    ja, ka = lax.axis_index("ja"), lax.axis_index("ka")
    z, c = ja // 2, ja % 2
    sib = z * 2 + (1 - c)
    loads = [
        pltpu.make_async_copy(src, dst, load_sem.at[i])
        for i, (src, dst) in enumerate(((tensor, x_v), (factor_one, f1_v), (factor_two, f2_v)))
    ]
    for load in loads:
        load.start()

    barrier = pltpu.get_barrier_semaphore()

    x, y = ka // 4, ka % 4
    x_next = [((x + step) % 4) * 4 + y for step in (1, 3)]
    y_next = [x * 4 + (y + step) % 4 for step in (1, 3)]

    def greet_ja(d, carry):
        pl.semaphore_signal(barrier, inc=1, device_id={"ja": (ja + d) % n_ja}, device_id_type=MESH)
        return carry

    def greet_ka(d, carry):
        pl.semaphore_signal(barrier, inc=1, device_id={"ka": (ka + d) % n_ka}, device_id_type=MESH)
        return carry

    lax.fori_loop(1, n_ja, greet_ja, 0)
    lax.fori_loop(1, n_ka, greet_ka, 0)

    for load in loads:
        load.wait()
    x_hi, x_lo = hi_lo(x_v[...].reshape(256, 1024))
    f_hi, f_lo = hi_lo(f1_v[...])
    mine = jnp.dot(x_hi, f_hi, preferred_element_type=F32)
    mine += jnp.dot(x_hi, f_lo, preferred_element_type=F32)
    mine += jnp.dot(x_lo, f_hi, preferred_element_type=F32)
    own_row = pl.multiple_of(ja * 64, 64)
    core[:, pl.ds(own_row, 64), :] = mine.astype(BF16).reshape(4, 64, 256)
    f2_out[...] = f2_v[...].astype(F32).T.astype(BF16).reshape(n_ja, 16, 64)
    f2_in[pl.ds(ja, 1)] = f2_out[pl.ds(ja, 1)]

    rhs[0:256] = x_hi
    rhs[256:512] = x_lo
    rhs[512:768] = x_hi
    for block in range(8):
        turned = x_v[:, :, block * 128 : (block + 1) * 128].reshape(256, 128).T
        t_hi, t_lo = hi_lo(turned)
        for half in range(2):
            rows = slice(half * 64, (half + 1) * 64)
            lhs[half, block, :, 0:256] = t_hi[rows]
            lhs[half, block, :, 256:512] = t_hi[rows]
            lhs[half, block, :, 512:768] = t_lo[rows]

    def product(half):
        left = lhs[half].reshape(512, 768)
        for block in range(4):
            columns = slice(block * 256, (block + 1) * 256)
            part[:, :, columns] = jnp.dot(left, rhs[:, columns], preferred_element_type=F32).reshape(8, 64, 256)

    def rows_of(m):
        at = pl.ds(pl.multiple_of(m * 8, 8), 8)
        low_a, high_a = groups_of_four([part[i, at, :] for i in range(4)])
        low_b, high_b = groups_of_four([part[4 + i, at, :] for i in range(4)])
        return (
            jnp.concatenate([low_a[0], low_b[0]], axis=0),
            jnp.concatenate([high_a[0], high_b[0]], axis=0),
        )

    def half_copy(m):
        return pltpu.make_async_remote_copy(
            to_sib.at[m], from_sib.at[m], half_send.at[m], half_recv.at[m],
            device_id={"ja": sib}, device_id_type=MESH,
        )

    product(1 - c)

    def give(row):
        def body(h, carry):
            m = row * 2 + h
            low, high = rows_of(m)
            to_sib[m, 0] = low.astype(BF16)
            to_sib[m, 1] = high.astype(BF16)
            return carry

        lax.fori_loop(0, 2, body, 0)

    for step in (2, 1, 3, 0):
        give((x + step) % 4)
    product(c)

    pl.semaphore_wait(barrier, n_ja + n_ka - 2)

    def block_of(chunk, source_z, source_c):
        row = pl.multiple_of(source_z * 128 + source_c * 64, 64)
        return core.at[chunk, pl.ds(row, 64), :]

    def ring_copy(up, chunk, hop):
        source = (z - (hop - 1) + n_z) % n_z if up else (z + (hop - 1)) % n_z
        target = (z + 1) % n_z if up else (z - 1 + n_z) % n_z
        block = block_of(chunk, source, c)
        send, recv = (up_send, up_recv) if up else (down_send, down_recv)
        return pltpu.make_async_remote_copy(
            block, block, send.at[chunk, hop - 1], recv.at[chunk, hop - 1],
            device_id={"ja": target * 2 + c}, device_id_type=MESH,
        )

    def arrival(up, chunk, hop):
        source = (z - hop + n_z) % n_z if up else (z + hop) % n_z
        block = block_of(chunk, source, c)
        send, recv = (up_send, up_recv) if up else (down_send, down_recv)
        return pltpu.make_async_remote_copy(
            block, block, send.at[chunk, hop - 1], recv.at[chunk, hop - 1],
            device_id={"ja": sib}, device_id_type=MESH,
        )

    def sib_copy(chunk, source_z, slot, source_c):
        block = block_of(chunk, source_z, source_c)
        return pltpu.make_async_remote_copy(
            block, block, sib_send.at[chunk, slot], sib_recv.at[chunk, slot],
            device_id={"ja": sib}, device_id_type=MESH,
        )

    def last_hop(up, chunk):
        return 4 if up == (chunk < 2) else 3

    order = [(up, chunk) for pair in zip((0, 1, 2, 3), (2, 3, 0, 1)) for up, chunk in zip((True, False), pair)]
    for up, chunk in order:
        ring_copy(up, chunk, 1).start()

    def pass_on(hop):
        for up, chunk in order:
            if hop > last_hop(up, chunk):
                continue
            arrival(up, chunk, hop).wait_recv()
            if hop < last_hop(up, chunk):
                ring_copy(up, chunk, hop + 1).start()
            source = (z - hop + n_z) % n_z if up else (z + hop) % n_z
            sib_copy(chunk, source, hop if up else n_z - hop, c).start()

    def f2_copy(d):
        to = (ja + d) % n_ja
        return pltpu.make_async_remote_copy(
            f2_out.at[to], f2_in.at[ja], f2_send.at[to], f2_recv.at[ja],
            device_id={"ja": to}, device_id_type=MESH,
        )

    def f2_arrival(d):
        source = (ja + d) % n_ja
        return pltpu.make_async_remote_copy(
            f2_out.at[source], f2_in.at[source], f2_send.at[source], f2_recv.at[source],
            device_id={"ja": source}, device_id_type=MESH,
        )

    def start_f2(d, carry):
        f2_copy(d).start()
        return carry

    def start_half(h, carry):
        half_copy((x * 2 + 4 + h) % 8).start()
        return carry

    lax.fori_loop(0, 8, start_half, 0)
    lax.fori_loop(1, n_ja, start_f2, 0)
    for chunk in range(4):
        sib_copy(chunk, z, 0, c).start()
    def half_of(left, half):
        return slice(left + half * 256, left + (half + 1) * 256)

    def slab(axis, at, lanes):
        return (pl.ds(at, 1), slice(None), slice(None), lanes) if axis == 0 else (slice(None), pl.ds(at, 1), slice(None), lanes)

    def plane_copy(axis, way, kind):
        place = x if axis == 0 else y
        to = (place + (1, 3)[way]) % 4
        peer = (x_next, y_next)[axis][way]
        at = (place + 2) % 4 if kind == 0 else to
        half = 1 - way if kind == 1 else way
        lanes = half_of(axis * 512, half)
        source = to_plane.at[at, :, :, lanes] if axis == 0 else to_plane.at[:, at, :, lanes]
        target = far.at[axis, way] if kind == 0 else near.at[axis, way, :, :, half_of(0, half)]
        return pltpu.make_async_remote_copy(
            source, target, plane_send.at[axis, way, kind], plane_recv.at[axis, way, kind],
            device_id={"ka": peer}, device_id_type=MESH,
        )

    def cross_copy(axis, way, kind):
        place = y if axis == 0 else x
        to = (place + (1, 3)[way]) % 4
        peer = (y_next, x_next)[axis][way]
        at = (place + 2) % 4 if kind == 0 else to
        half = 1 - way if kind == 1 else way
        target = far_cross.at[axis, way] if kind == 0 else near_cross.at[axis, way, :, half_of(0, half)]
        return pltpu.make_async_remote_copy(
            to_cross.at[axis, at, :, half_of(0, half)], target,
            cross_send.at[axis, way, kind], cross_recv.at[axis, way, kind],
            device_id={"ka": peer}, device_id_type=MESH,
        )

    def combine(row):
        def body(h, carry):
            m = row * 2 + h
            half_copy(m).wait_recv()
            low, high = rows_of(m)
            to_plane[row, h * 2] = (low + from_sib[m, 0].astype(F32)).astype(BF16)
            to_plane[row, h * 2 + 1] = (high + from_sib[m, 1].astype(F32)).astype(BF16)
            return carry

        lax.fori_loop(0, 2, body, 0)

    combine((x + 2) % 4)
    for way in range(2):
        plane_copy(0, way, 0).start()
    combine((x + 1) % 4)
    plane_copy(0, 0, 1).start()
    combine((x + 3) % 4)
    plane_copy(0, 1, 1).start()
    combine(x)
    for kind in range(2):
        for way in range(2):
            plane_copy(1, way, kind).start()
    pass_on(1)

    for axis in range(2):
        place = x if axis == 0 else y
        for way in range(2):
            plane_copy(axis, way, 0).wait_recv()
            where = slab(axis, (place + (1, 3)[way]) % 4, half_of(axis * 512, way))
            mine = to_plane[where]
            to_plane[where] = (mine.astype(F32) + far[axis, way].reshape(mine.shape).astype(F32)).astype(BF16)
            plane_copy(axis, way, 2).start()
    pass_on(2)
    for axis in range(2):
        for way in range(2):
            for kind in (1, 2):
                plane_copy(axis, way, kind).wait_recv()
        mine = to_plane[slab(axis, x if axis == 0 else y, slice(axis * 512, axis * 512 + 512))].reshape(4, 32, 512)
        to_cross[axis] = (mine.astype(F32) + near[axis, 0].astype(F32) + near[axis, 1].astype(F32)).astype(BF16)
        for kind in range(2):
            for way in range(2):
                cross_copy(axis, way, kind).start()
    pass_on(3)
    pass_on(4)

    for slot in range(8):
        for chunk in range(4):
            sib_copy(chunk, (z - slot + n_z) % n_z, slot, 1 - c).wait_recv()

    own = core[:, pl.ds(own_row, 64), :]
    sums = []
    for block in range(4):
        columns = slice(block * 256, (block + 1) * 256)
        total = jnp.zeros((64, 256), F32)
        for k in range(4):
            total += lax.dot_general(
                own[k], core[k, columns, :], (((1,), (1,)), ((), ())), preferred_element_type=F32
            )
        sums.append(total)
    low, high = groups_of_four(sums)
    g2_out[:, 0] = low.astype(BF16)
    g2_out[:, 1] = high.astype(BF16)

    def g2_copy(to):
        return pltpu.make_async_remote_copy(
            g2_out.at[to // 2, to % 2], g2_in.at[ka], g2_send.at[to], g2_recv.at[ka],
            device_id={"ka": to}, device_id_type=MESH,
        )

    def g2_arrival(source):
        return pltpu.make_async_remote_copy(
            g2_out.at[source // 2, source % 2], g2_in.at[source], g2_send.at[source], g2_recv.at[source],
            device_id={"ka": source}, device_id_type=MESH,
        )

    def start_g2(d, carry):
        g2_copy((ka + d) % n_ka).start()
        return carry

    lax.fori_loop(1, n_ka, start_g2, 0)

    for axis in range(2):
        place = y if axis == 0 else x
        for way in range(2):
            cross_copy(axis, way, 0).wait_recv()
            where = (axis, (place + (1, 3)[way]) % 4, slice(None), half_of(0, way))
            to_cross[where] = (to_cross[where].astype(F32) + far_cross[axis, way].astype(F32)).astype(BF16)
            cross_copy(axis, way, 2).start()

    def end_f2(d, carry):
        f2_arrival(d).wait_recv()
        return carry

    lax.fori_loop(1, n_ja, end_f2, 0)
    f2 = jnp.concatenate([f2_in[i].astype(F32) for i in range(n_ja)], axis=1).astype(BF16)
    for k in range(4):
        reduced[k] = jnp.dot(f2, core[k], preferred_element_type=F32)

    sides = []
    for axis in range(2):
        for way in range(2):
            for kind in (1, 2):
                cross_copy(axis, way, kind).wait_recv()
        mine = to_cross[axis, y if axis == 0 else x]
        sides.append(mine.astype(F32) + near_cross[axis, 0].astype(F32) + near_cross[axis, 1].astype(F32))
    total = jnp.concatenate(sides, axis=1)
    low, high = groups_of_four([total[:, i * 256 : (i + 1) * 256] for i in range(4)])
    to_line[:, 0] = low.astype(BF16)
    to_line[:, 1] = high.astype(BF16)

    def line_copy(to):
        return pltpu.make_async_remote_copy(
            to_line.at[to // 2, to % 2], from_line.at[z], line_send.at[to], line_recv.at[z],
            device_id={"ja": to * 2 + c}, device_id_type=MESH,
        )

    def line_arrival(source):
        return pltpu.make_async_remote_copy(
            to_line.at[source // 2, source % 2], from_line.at[source], line_send.at[source],
            line_recv.at[source], device_id={"ja": source * 2 + c}, device_id_type=MESH,
        )

    def start_line(d, carry):
        line_copy((z + d) % n_z).start()
        return carry

    lax.fori_loop(1, n_z, start_line, 0)

    def add_g2(d, total):
        source = (ka + d) % n_ka
        g2_arrival(source).wait_recv()
        return total + g2_in[source].astype(F32)

    total = lax.fori_loop(1, n_ka, add_g2, g2_out[ka // 2, ka % 2].astype(F32)) * norms[1]
    for i in range(4):
        gram_two[:, i * 256 : (i + 1) * 256] = total[i * 4 : (i + 1) * 4]

    def add_line(d, total):
        source = (z + d) % n_z
        line_arrival(source).wait_recv()
        return total + from_line[source].astype(F32)

    total = lax.fori_loop(1, n_z, add_line, to_line[z // 2, z % 2].astype(F32)) * norms[0]
    for i in range(4):
        gram_one[:, i * 256 : (i + 1) * 256] = total[i * 4 : (i + 1) * 4]

    for chunk in range(4):
        for up in (True, False):
            for hop in range(1, last_hop(up, chunk) + 1):
                ring_copy(up, chunk, hop).wait_send()
        for slot in range(8):
            sib_copy(chunk, (z - slot + n_z) % n_z, slot, c).wait_send()
    for axis in range(2):
        for way in range(2):
            for kind in range(3):
                plane_copy(axis, way, kind).wait_send()
                cross_copy(axis, way, kind).wait_send()

    def end_ja(d, carry):
        f2_copy(d).wait_send()
        return carry

    def end_ka(d, carry):
        g2_copy((ka + d) % n_ka).wait_send()
        return carry

    def end_z(d, carry):
        line_copy((z + d) % n_z).wait_send()
        return carry

    def end_half(m, carry):
        half_copy(m).wait_send()
        return carry

    lax.fori_loop(1, n_ja, end_ja, 0)
    lax.fori_loop(1, n_ka, end_ka, 0)
    lax.fori_loop(1, n_z, end_z, 0)
    lax.fori_loop(0, 8, end_half, 0)


def solution(mesh):
    n_ja, n_ka = mesh.shape["ja"], mesh.shape["ka"]

    def shards(tensor, factor_one, factor_two):
        slices, owned, width = tensor.shape
        norm_one = 1.0 / math.sqrt(owned * n_ja * slices * n_ka)
        norm_two = 1.0 / math.sqrt(slices * n_ka * factor_one.shape[1])
        dma = pltpu.SemaphoreType.DMA

        def body(*refs):
            kernel((norm_one, norm_two), (n_ja, n_ka), *refs)

        return pl.pallas_call(
            body,
            out_shape=(
                jax.ShapeDtypeStruct((4, 1024), F32),
                jax.ShapeDtypeStruct((4, 1024), F32),
                jax.ShapeDtypeStruct((4, 16, 256), F32),
            ),
            in_specs=[pl.BlockSpec(memory_space=pl.ANY)] * 3,
            out_specs=[pl.BlockSpec(memory_space=pltpu.VMEM)] * 3,
            scratch_shapes=[
                pltpu.VMEM((4, 64, 1024), F32),
                pltpu.VMEM((1024, 256), F32),
                pltpu.VMEM((64, 256), BF16),
                pltpu.VMEM((2, 8, 64, 768), BF16),
                pltpu.VMEM((768, 1024), BF16),
                pltpu.VMEM((8, 64, 1024), F32),
                pltpu.VMEM((8, 2, 32, 1024), BF16),
                pltpu.VMEM((8, 2, 32, 1024), BF16),
                pltpu.VMEM((4, 4, 32, 1024), BF16),
                pltpu.VMEM((2, 2, 4, 32, 256), BF16),
                pltpu.VMEM((2, 2, 4, 32, 512), BF16),
                pltpu.VMEM((2, 4, 32, 512), BF16),
                pltpu.VMEM((2, 2, 32, 256), BF16),
                pltpu.VMEM((2, 2, 32, 512), BF16),
                pltpu.VMEM((4, 2, 16, 256), BF16),
                pltpu.VMEM((8, 16, 256), BF16),
                pltpu.VMEM((4, 1024, 256), BF16),
                pltpu.VMEM((16, 16, 64), BF16),
                pltpu.VMEM((16, 16, 64), BF16),
                pltpu.VMEM((8, 2, 16, 256), BF16),
                pltpu.VMEM((16, 16, 256), BF16),
                dma((3,)),
                dma((4, 4)), dma((4, 4)), dma((4, 4)), dma((4, 4)),
                dma((4, 8)), dma((4, 8)),
                dma((8,)), dma((8,)),
                dma((2, 2, 3)), dma((2, 2, 3)),
                dma((2, 2, 3)), dma((2, 2, 3)),
                dma((8,)), dma((8,)),
                dma((16,)), dma((16,)),
                dma((16,)), dma((16,)),
            ],
            compiler_params=pltpu.CompilerParams(
                collective_id=0, has_side_effects=True, vmem_limit_bytes=48 * 1024 * 1024
            ),
        )(tensor, factor_one, factor_two)

    return jax.shard_map(
        shards,
        mesh=mesh,
        in_specs=(P("ka", "ja", None), P(), P("ja", None)),
        out_specs=(P(("ja", "ka"), None), P(("ja", "ka"), None), P("ka", "ja", None)),
        check_vma=False,
    )
```

```python
import math

import jax
import jax.numpy as jnp
from jax import lax
from jax.experimental import pallas as pl
from jax.experimental.pallas import tpu as pltpu
from jax.sharding import PartitionSpec as P

MESH = pl.DeviceIdType.MESH
F32 = jnp.float32
BF16 = jnp.bfloat16


def hi_lo(x):
    hi = x.astype(BF16)
    return hi, (x - hi.astype(F32)).astype(BF16)


def groups_of_four(parts):
    rows, width = parts[0].shape
    n = rows // 8
    first = lax.broadcasted_iota(jnp.int32, (n, 8, width), 1) < 4

    def pair(a, b):
        a, b = a.reshape(n, 8, width), b.reshape(n, 8, width)
        low = jnp.where(first, a, pltpu.roll(b, 4, axis=1))
        high = jnp.where(first, pltpu.roll(a, 4, axis=1), b)
        return low, high

    low_a, high_a = pair(parts[0], parts[1])
    low_b, high_b = pair(parts[2], parts[3])
    return jnp.concatenate([low_a, low_b], axis=1), jnp.concatenate([high_a, high_b], axis=1)


def kernel(
    norms, sizes, tensor, factor_one, factor_two, gram_one, gram_two, reduced,
    x_v, f1_v, f2_v, lhs, rhs, part, to_sib, from_sib, to_plane, far, near, to_cross, far_cross, near_cross,
    to_line, from_line, core, f2_out, f2_in, g2_out, g2_in,
    load_sem, up_send, up_recv, down_send, down_recv, sib_send, sib_recv, half_send, half_recv,
    plane_send, plane_recv, cross_send, cross_recv, line_send, line_recv, f2_send, f2_recv, g2_send, g2_recv,
):
    n_ja, n_ka = sizes
    n_z = n_ja // 2
    ja, ka = lax.axis_index("ja"), lax.axis_index("ka")
    z, c = ja // 2, ja % 2
    sib = z * 2 + (1 - c)
    loads = [
        pltpu.make_async_copy(src, dst, load_sem.at[i])
        for i, (src, dst) in enumerate(((tensor, x_v), (factor_one, f1_v), (factor_two, f2_v)))
    ]
    for load in loads:
        load.start()

    barrier = pltpu.get_barrier_semaphore()

    x, y = ka // 4, ka % 4
    x_next = [((x + step) % 4) * 4 + y for step in (1, 3)]
    y_next = [x * 4 + (y + step) % 4 for step in (1, 3)]

    def greet_ja(d, carry):
        pl.semaphore_signal(barrier, inc=1, device_id={"ja": (ja + d) % n_ja}, device_id_type=MESH)
        return carry

    def greet_ka(d, carry):
        pl.semaphore_signal(barrier, inc=1, device_id={"ka": (ka + d) % n_ka}, device_id_type=MESH)
        return carry

    lax.fori_loop(1, n_ja, greet_ja, 0)
    lax.fori_loop(1, n_ka, greet_ka, 0)

    for load in loads:
        load.wait()
    x_hi, x_lo = hi_lo(x_v[...].reshape(256, 1024))
    f_hi, f_lo = hi_lo(f1_v[...])
    mine = jnp.dot(x_hi, f_hi, preferred_element_type=F32)
    mine += jnp.dot(x_hi, f_lo, preferred_element_type=F32)
    mine += jnp.dot(x_lo, f_hi, preferred_element_type=F32)
    own_row = pl.multiple_of(ja * 64, 64)
    core[:, pl.ds(own_row, 64), :] = mine.astype(BF16).reshape(4, 64, 256)
    f2_out[...] = f2_v[...].astype(F32).T.astype(BF16).reshape(n_ja, 16, 64)
    f2_in[pl.ds(ja, 1)] = f2_out[pl.ds(ja, 1)]

    rhs[0:256] = x_hi
    rhs[256:512] = x_lo
    rhs[512:768] = x_hi
    for block in range(8):
        turned = x_v[:, :, block * 128 : (block + 1) * 128].reshape(256, 128).T
        t_hi, t_lo = hi_lo(turned)
        for half in range(2):
            rows = slice(half * 64, (half + 1) * 64)
            lhs[half, block, :, 0:256] = t_hi[rows]
            lhs[half, block, :, 256:512] = t_hi[rows]
            lhs[half, block, :, 512:768] = t_lo[rows]

    def product(half):
        left = lhs[half].reshape(512, 768)
        for block in range(4):
            columns = slice(block * 256, (block + 1) * 256)
            part[:, :, columns] = jnp.dot(left, rhs[:, columns], preferred_element_type=F32).reshape(8, 64, 256)

    def rows_of(m):
        at = pl.ds(pl.multiple_of(m * 8, 8), 8)
        low_a, high_a = groups_of_four([part[i, at, :] for i in range(4)])
        low_b, high_b = groups_of_four([part[4 + i, at, :] for i in range(4)])
        return (
            jnp.concatenate([low_a[0], low_b[0]], axis=0),
            jnp.concatenate([high_a[0], high_b[0]], axis=0),
        )

    def half_copy(m):
        return pltpu.make_async_remote_copy(
            to_sib.at[m], from_sib.at[m], half_send.at[m], half_recv.at[m],
            device_id={"ja": sib}, device_id_type=MESH,
        )

    product(1 - c)

    def give(row):
        def body(h, carry):
            m = row * 2 + h
            low, high = rows_of(m)
            to_sib[m, 0] = low.astype(BF16)
            to_sib[m, 1] = high.astype(BF16)
            return carry

        lax.fori_loop(0, 2, body, 0)

    for step in (2, 1, 3, 0):
        give((x + step) % 4)
    product(c)

    pl.semaphore_wait(barrier, n_ja + n_ka - 2)

    def block_of(chunk, source_z, source_c):
        row = pl.multiple_of(source_z * 128 + source_c * 64, 64)
        return core.at[chunk, pl.ds(row, 64), :]

    def ring_copy(up, chunk, hop):
        source = (z - (hop - 1) + n_z) % n_z if up else (z + (hop - 1)) % n_z
        target = (z + 1) % n_z if up else (z - 1 + n_z) % n_z
        block = block_of(chunk, source, c)
        send, recv = (up_send, up_recv) if up else (down_send, down_recv)
        return pltpu.make_async_remote_copy(
            block, block, send.at[chunk, hop - 1], recv.at[chunk, hop - 1],
            device_id={"ja": target * 2 + c}, device_id_type=MESH,
        )

    def arrival(up, chunk, hop):
        source = (z - hop + n_z) % n_z if up else (z + hop) % n_z
        block = block_of(chunk, source, c)
        send, recv = (up_send, up_recv) if up else (down_send, down_recv)
        return pltpu.make_async_remote_copy(
            block, block, send.at[chunk, hop - 1], recv.at[chunk, hop - 1],
            device_id={"ja": sib}, device_id_type=MESH,
        )

    def sib_copy(chunk, source_z, slot, source_c):
        block = block_of(chunk, source_z, source_c)
        return pltpu.make_async_remote_copy(
            block, block, sib_send.at[chunk, slot], sib_recv.at[chunk, slot],
            device_id={"ja": sib}, device_id_type=MESH,
        )

    def last_hop(up, chunk):
        return 4 if up == (chunk < 2) else 3

    order = [(up, chunk) for pair in zip((0, 1, 2, 3), (2, 3, 0, 1)) for up, chunk in zip((True, False), pair)]
    for up, chunk in order:
        ring_copy(up, chunk, 1).start()

    def pass_on(hop):
        for up, chunk in order:
            if hop > last_hop(up, chunk):
                continue
            arrival(up, chunk, hop).wait_recv()
            if hop < last_hop(up, chunk):
                ring_copy(up, chunk, hop + 1).start()
            source = (z - hop + n_z) % n_z if up else (z + hop) % n_z
            sib_copy(chunk, source, hop if up else n_z - hop, c).start()

    def f2_copy(d):
        to = (ja + d) % n_ja
        return pltpu.make_async_remote_copy(
            f2_out.at[to], f2_in.at[ja], f2_send.at[to], f2_recv.at[ja],
            device_id={"ja": to}, device_id_type=MESH,
        )

    def f2_arrival(d):
        source = (ja + d) % n_ja
        return pltpu.make_async_remote_copy(
            f2_out.at[source], f2_in.at[source], f2_send.at[source], f2_recv.at[source],
            device_id={"ja": source}, device_id_type=MESH,
        )

    def start_f2(d, carry):
        f2_copy(d).start()
        return carry

    def start_half(h, carry):
        half_copy((x * 2 + 4 + h) % 8).start()
        return carry

    lax.fori_loop(0, 8, start_half, 0)
    lax.fori_loop(1, n_ja, start_f2, 0)
    for chunk in range(4):
        sib_copy(chunk, z, 0, c).start()
    def half_of(left, half):
        return slice(left + half * 256, left + (half + 1) * 256)

    def slab(axis, at, lanes):
        return (pl.ds(at, 1), slice(None), slice(None), lanes) if axis == 0 else (slice(None), pl.ds(at, 1), slice(None), lanes)

    def plane_copy(axis, way, kind):
        place = x if axis == 0 else y
        to = (place + (1, 3)[way]) % 4
        peer = (x_next, y_next)[axis][way]
        at = (place + 2) % 4 if kind == 0 else to
        half = 1 - way if kind == 1 else way
        lanes = half_of(axis * 512, half)
        source = to_plane.at[at, :, :, lanes] if axis == 0 else to_plane.at[:, at, :, lanes]
        target = far.at[axis, way] if kind == 0 else near.at[axis, way, :, :, half_of(0, half)]
        return pltpu.make_async_remote_copy(
            source, target, plane_send.at[axis, way, kind], plane_recv.at[axis, way, kind],
            device_id={"ka": peer}, device_id_type=MESH,
        )

    def cross_copy(axis, way, kind):
        place = y if axis == 0 else x
        to = (place + (1, 3)[way]) % 4
        peer = (y_next, x_next)[axis][way]
        at = (place + 2) % 4 if kind == 0 else to
        half = 1 - way if kind == 1 else way
        target = far_cross.at[axis, way] if kind == 0 else near_cross.at[axis, way, :, half_of(0, half)]
        return pltpu.make_async_remote_copy(
            to_cross.at[axis, at, :, half_of(0, half)], target,
            cross_send.at[axis, way, kind], cross_recv.at[axis, way, kind],
            device_id={"ka": peer}, device_id_type=MESH,
        )

    def combine(row):
        def body(h, carry):
            m = row * 2 + h
            half_copy(m).wait_recv()
            low, high = rows_of(m)
            to_plane[row, h * 2] = (low + from_sib[m, 0].astype(F32)).astype(BF16)
            to_plane[row, h * 2 + 1] = (high + from_sib[m, 1].astype(F32)).astype(BF16)
            return carry

        lax.fori_loop(0, 2, body, 0)

    combine((x + 2) % 4)
    for way in range(2):
        plane_copy(0, way, 0).start()
    combine((x + 1) % 4)
    plane_copy(0, 0, 1).start()
    combine((x + 3) % 4)
    plane_copy(0, 1, 1).start()
    combine(x)
    for kind in range(2):
        for way in range(2):
            plane_copy(1, way, kind).start()
    pass_on(1)

    for axis in range(2):
        place = x if axis == 0 else y
        for way in range(2):
            plane_copy(axis, way, 0).wait_recv()
            where = slab(axis, (place + (1, 3)[way]) % 4, half_of(axis * 512, way))
            mine = to_plane[where]
            to_plane[where] = (mine.astype(F32) + far[axis, way].reshape(mine.shape).astype(F32)).astype(BF16)
            plane_copy(axis, way, 2).start()
    pass_on(2)
    for axis in range(2):
        for way in range(2):
            for kind in (1, 2):
                plane_copy(axis, way, kind).wait_recv()
        mine = to_plane[slab(axis, x if axis == 0 else y, slice(axis * 512, axis * 512 + 512))].reshape(4, 32, 512)
        to_cross[axis] = (mine.astype(F32) + near[axis, 0].astype(F32) + near[axis, 1].astype(F32)).astype(BF16)
        for kind in range(2):
            for way in range(2):
                cross_copy(axis, way, kind).start()
    pass_on(3)
    pass_on(4)

    for axis in range(2):
        place = y if axis == 0 else x
        for way in range(2):
            cross_copy(axis, way, 0).wait_recv()
            where = (axis, (place + (1, 3)[way]) % 4, slice(None), half_of(0, way))
            to_cross[where] = (to_cross[where].astype(F32) + far_cross[axis, way].astype(F32)).astype(BF16)
            cross_copy(axis, way, 2).start()

    for slot in range(8):
        for chunk in range(4):
            sib_copy(chunk, (z - slot + n_z) % n_z, slot, 1 - c).wait_recv()

    sides = []
    for axis in range(2):
        for way in range(2):
            for kind in (1, 2):
                cross_copy(axis, way, kind).wait_recv()
        mine = to_cross[axis, y if axis == 0 else x]
        sides.append(mine.astype(F32) + near_cross[axis, 0].astype(F32) + near_cross[axis, 1].astype(F32))
    total = jnp.concatenate(sides, axis=1)
    low, high = groups_of_four([total[:, i * 256 : (i + 1) * 256] for i in range(4)])
    to_line[:, 0] = low.astype(BF16)
    to_line[:, 1] = high.astype(BF16)

    def line_copy(to):
        return pltpu.make_async_remote_copy(
            to_line.at[to // 2, to % 2], from_line.at[z], line_send.at[to], line_recv.at[z],
            device_id={"ja": to * 2 + c}, device_id_type=MESH,
        )

    def line_arrival(source):
        return pltpu.make_async_remote_copy(
            to_line.at[source // 2, source % 2], from_line.at[source], line_send.at[source],
            line_recv.at[source], device_id={"ja": source * 2 + c}, device_id_type=MESH,
        )

    def start_line(d, carry):
        line_copy((z + d) % n_z).start()
        return carry

    lax.fori_loop(1, n_z, start_line, 0)

    own = core[:, pl.ds(own_row, 64), :]
    sums = []
    for block in range(4):
        columns = slice(block * 256, (block + 1) * 256)
        total = jnp.zeros((64, 256), F32)
        for k in range(4):
            total += lax.dot_general(
                own[k], core[k, columns, :], (((1,), (1,)), ((), ())), preferred_element_type=F32
            )
        sums.append(total)
    low, high = groups_of_four(sums)
    g2_out[:, 0] = low.astype(BF16)
    g2_out[:, 1] = high.astype(BF16)

    def g2_copy(to):
        return pltpu.make_async_remote_copy(
            g2_out.at[to // 2, to % 2], g2_in.at[ka], g2_send.at[to], g2_recv.at[ka],
            device_id={"ka": to}, device_id_type=MESH,
        )

    def g2_arrival(source):
        return pltpu.make_async_remote_copy(
            g2_out.at[source // 2, source % 2], g2_in.at[source], g2_send.at[source], g2_recv.at[source],
            device_id={"ka": source}, device_id_type=MESH,
        )

    def start_g2(d, carry):
        g2_copy((ka + d) % n_ka).start()
        return carry

    lax.fori_loop(1, n_ka, start_g2, 0)

    def end_f2(d, carry):
        f2_arrival(d).wait_recv()
        return carry

    lax.fori_loop(1, n_ja, end_f2, 0)
    f2 = jnp.concatenate([f2_in[i].astype(F32) for i in range(n_ja)], axis=1).astype(BF16)
    for k in range(4):
        reduced[k] = jnp.dot(f2, core[k], preferred_element_type=F32)

    def add_g2(d, total):
        source = (ka + d) % n_ka
        g2_arrival(source).wait_recv()
        return total + g2_in[source].astype(F32)

    total = lax.fori_loop(1, n_ka, add_g2, g2_out[ka // 2, ka % 2].astype(F32)) * norms[1]
    for i in range(4):
        gram_two[:, i * 256 : (i + 1) * 256] = total[i * 4 : (i + 1) * 4]

    def add_line(d, total):
        source = (z + d) % n_z
        line_arrival(source).wait_recv()
        return total + from_line[source].astype(F32)

    total = lax.fori_loop(1, n_z, add_line, to_line[z // 2, z % 2].astype(F32)) * norms[0]
    for i in range(4):
        gram_one[:, i * 256 : (i + 1) * 256] = total[i * 4 : (i + 1) * 4]

    for chunk in range(4):
        for up in (True, False):
            for hop in range(1, last_hop(up, chunk) + 1):
                ring_copy(up, chunk, hop).wait_send()
        for slot in range(8):
            sib_copy(chunk, (z - slot + n_z) % n_z, slot, c).wait_send()
    for axis in range(2):
        for way in range(2):
            for kind in range(3):
                plane_copy(axis, way, kind).wait_send()
                cross_copy(axis, way, kind).wait_send()

    def end_ja(d, carry):
        f2_copy(d).wait_send()
        return carry

    def end_ka(d, carry):
        g2_copy((ka + d) % n_ka).wait_send()
        return carry

    def end_z(d, carry):
        line_copy((z + d) % n_z).wait_send()
        return carry

    def end_half(m, carry):
        half_copy(m).wait_send()
        return carry

    lax.fori_loop(1, n_ja, end_ja, 0)
    lax.fori_loop(1, n_ka, end_ka, 0)
    lax.fori_loop(1, n_z, end_z, 0)
    lax.fori_loop(0, 8, end_half, 0)


def solution(mesh):
    n_ja, n_ka = mesh.shape["ja"], mesh.shape["ka"]

    def shards(tensor, factor_one, factor_two):
        slices, owned, width = tensor.shape
        norm_one = 1.0 / math.sqrt(owned * n_ja * slices * n_ka)
        norm_two = 1.0 / math.sqrt(slices * n_ka * factor_one.shape[1])
        dma = pltpu.SemaphoreType.DMA

        def body(*refs):
            kernel((norm_one, norm_two), (n_ja, n_ka), *refs)

        return pl.pallas_call(
            body,
            out_shape=(
                jax.ShapeDtypeStruct((4, 1024), F32),
                jax.ShapeDtypeStruct((4, 1024), F32),
                jax.ShapeDtypeStruct((4, 16, 256), F32),
            ),
            in_specs=[pl.BlockSpec(memory_space=pl.ANY)] * 3,
            out_specs=[pl.BlockSpec(memory_space=pltpu.VMEM)] * 3,
            scratch_shapes=[
                pltpu.VMEM((4, 64, 1024), F32),
                pltpu.VMEM((1024, 256), F32),
                pltpu.VMEM((64, 256), BF16),
                pltpu.VMEM((2, 8, 64, 768), BF16),
                pltpu.VMEM((768, 1024), BF16),
                pltpu.VMEM((8, 64, 1024), F32),
                pltpu.VMEM((8, 2, 32, 1024), BF16),
                pltpu.VMEM((8, 2, 32, 1024), BF16),
                pltpu.VMEM((4, 4, 32, 1024), BF16),
                pltpu.VMEM((2, 2, 4, 32, 256), BF16),
                pltpu.VMEM((2, 2, 4, 32, 512), BF16),
                pltpu.VMEM((2, 4, 32, 512), BF16),
                pltpu.VMEM((2, 2, 32, 256), BF16),
                pltpu.VMEM((2, 2, 32, 512), BF16),
                pltpu.VMEM((4, 2, 16, 256), BF16),
                pltpu.VMEM((8, 16, 256), BF16),
                pltpu.VMEM((4, 1024, 256), BF16),
                pltpu.VMEM((16, 16, 64), BF16),
                pltpu.VMEM((16, 16, 64), BF16),
                pltpu.VMEM((8, 2, 16, 256), BF16),
                pltpu.VMEM((16, 16, 256), BF16),
                dma((3,)),
                dma((4, 4)), dma((4, 4)), dma((4, 4)), dma((4, 4)),
                dma((4, 8)), dma((4, 8)),
                dma((8,)), dma((8,)),
                dma((2, 2, 3)), dma((2, 2, 3)),
                dma((2, 2, 3)), dma((2, 2, 3)),
                dma((8,)), dma((8,)),
                dma((16,)), dma((16,)),
                dma((16,)), dma((16,)),
            ],
            compiler_params=pltpu.CompilerParams(
                collective_id=0, has_side_effects=True, vmem_limit_bytes=48 * 1024 * 1024
            ),
        )(tensor, factor_one, factor_two)

    return jax.shard_map(
        shards,
        mesh=mesh,
        in_specs=(P("ka", "ja", None), P(), P("ja", None)),
        out_specs=(P(("ja", "ka"), None), P(("ja", "ka"), None), P("ka", "ja", None)),
        check_vma=False,
    )
```

```python
import math

import jax
import jax.numpy as jnp
from jax import lax
from jax.experimental import pallas as pl
from jax.experimental.pallas import tpu as pltpu
from jax.sharding import PartitionSpec as P

MESH = pl.DeviceIdType.MESH
F32 = jnp.float32
BF16 = jnp.bfloat16


def hi_lo(x):
    hi = x.astype(BF16)
    return hi, (x - hi.astype(F32)).astype(BF16)


def groups_of_four(parts):
    rows, width = parts[0].shape
    n = rows // 8
    first = lax.broadcasted_iota(jnp.int32, (n, 8, width), 1) < 4

    def pair(a, b):
        a, b = a.reshape(n, 8, width), b.reshape(n, 8, width)
        low = jnp.where(first, a, pltpu.roll(b, 4, axis=1))
        high = jnp.where(first, pltpu.roll(a, 4, axis=1), b)
        return low, high

    low_a, high_a = pair(parts[0], parts[1])
    low_b, high_b = pair(parts[2], parts[3])
    return jnp.concatenate([low_a, low_b], axis=1), jnp.concatenate([high_a, high_b], axis=1)


def kernel(
    norms, sizes, tensor, factor_one, factor_two, gram_one, gram_two, reduced,
    x_v, f1_v, f2_v, lhs, rhs, part, to_sib, from_sib, to_plane, far, near, to_cross, far_cross, near_cross,
    to_line, from_line, core, f2_out, f2_in, g2_out, g2_in,
    load_sem, up_send, up_recv, down_send, down_recv, sib_send, sib_recv, half_send, half_recv,
    plane_send, plane_recv, cross_send, cross_recv, line_send, line_recv, f2_send, f2_recv, g2_send, g2_recv,
):
    n_ja, n_ka = sizes
    n_z = n_ja // 2
    ja, ka = lax.axis_index("ja"), lax.axis_index("ka")
    z, c = ja // 2, ja % 2
    sib = z * 2 + (1 - c)
    loads = [
        pltpu.make_async_copy(src, dst, load_sem.at[i])
        for i, (src, dst) in enumerate(((tensor, x_v), (factor_one, f1_v), (factor_two, f2_v)))
    ]
    for load in loads:
        load.start()

    barrier = pltpu.get_barrier_semaphore()

    x, y = ka // 4, ka % 4
    x_next = [((x + step) % 4) * 4 + y for step in (1, 3)]
    y_next = [x * 4 + (y + step) % 4 for step in (1, 3)]

    def greet_ja(d, carry):
        pl.semaphore_signal(barrier, inc=1, device_id={"ja": (ja + d) % n_ja}, device_id_type=MESH)
        return carry

    def greet_ka(d, carry):
        pl.semaphore_signal(barrier, inc=1, device_id={"ka": (ka + d) % n_ka}, device_id_type=MESH)
        return carry

    lax.fori_loop(1, n_ja, greet_ja, 0)
    lax.fori_loop(1, n_ka, greet_ka, 0)

    for load in loads:
        load.wait()
    x_hi, x_lo = hi_lo(x_v[...].reshape(256, 1024))
    f_hi, f_lo = hi_lo(f1_v[...])
    mine = jnp.dot(x_hi, f_hi, preferred_element_type=F32)
    mine += jnp.dot(x_hi, f_lo, preferred_element_type=F32)
    mine += jnp.dot(x_lo, f_hi, preferred_element_type=F32)
    own_row = pl.multiple_of(ja * 64, 64)
    core[:, pl.ds(own_row, 64), :] = mine.astype(BF16).reshape(4, 64, 256)
    f2_out[...] = f2_v[...].astype(F32).T.astype(BF16).reshape(n_ja, 16, 64)
    f2_in[pl.ds(ja, 1)] = f2_out[pl.ds(ja, 1)]

    rhs[0:256] = x_hi
    rhs[256:512] = x_lo
    rhs[512:768] = x_hi
    for block in range(8):
        turned = x_v[:, :, block * 128 : (block + 1) * 128].reshape(256, 128).T
        t_hi, t_lo = hi_lo(turned)
        for half in range(2):
            rows = slice(half * 64, (half + 1) * 64)
            lhs[half, block, :, 0:256] = t_hi[rows]
            lhs[half, block, :, 256:512] = t_hi[rows]
            lhs[half, block, :, 512:768] = t_lo[rows]

    def product(half):
        left = lhs[half].reshape(512, 768)
        for block in range(4):
            columns = slice(block * 256, (block + 1) * 256)
            part[:, :, columns] = jnp.dot(left, rhs[:, columns], preferred_element_type=F32).reshape(8, 64, 256)

    def rows_of(m):
        at = pl.ds(pl.multiple_of(m * 8, 8), 8)
        low_a, high_a = groups_of_four([part[i, at, :] for i in range(4)])
        low_b, high_b = groups_of_four([part[4 + i, at, :] for i in range(4)])
        return (
            jnp.concatenate([low_a[0], low_b[0]], axis=0),
            jnp.concatenate([high_a[0], high_b[0]], axis=0),
        )

    def half_copy(m):
        return pltpu.make_async_remote_copy(
            to_sib.at[m], from_sib.at[m], half_send.at[m], half_recv.at[m],
            device_id={"ja": sib}, device_id_type=MESH,
        )

    product(1 - c)

    def give(row):
        def body(h, carry):
            m = row * 2 + h
            low, high = rows_of(m)
            to_sib[m, 0] = low.astype(BF16)
            to_sib[m, 1] = high.astype(BF16)
            return carry

        lax.fori_loop(0, 2, body, 0)

    for step in (2, 1, 3, 0):
        give((x + step) % 4)
    product(c)

    pl.semaphore_wait(barrier, n_ja + n_ka - 2)

    def block_of(chunk, source_z, source_c):
        row = pl.multiple_of(source_z * 128 + source_c * 64, 64)
        return core.at[chunk, pl.ds(row, 64), :]

    def ring_copy(up, chunk, hop):
        source = (z - (hop - 1) + n_z) % n_z if up else (z + (hop - 1)) % n_z
        target = (z + 1) % n_z if up else (z - 1 + n_z) % n_z
        block = block_of(chunk, source, c)
        send, recv = (up_send, up_recv) if up else (down_send, down_recv)
        return pltpu.make_async_remote_copy(
            block, block, send.at[chunk, hop - 1], recv.at[chunk, hop - 1],
            device_id={"ja": target * 2 + c}, device_id_type=MESH,
        )

    def arrival(up, chunk, hop):
        source = (z - hop + n_z) % n_z if up else (z + hop) % n_z
        block = block_of(chunk, source, c)
        send, recv = (up_send, up_recv) if up else (down_send, down_recv)
        return pltpu.make_async_remote_copy(
            block, block, send.at[chunk, hop - 1], recv.at[chunk, hop - 1],
            device_id={"ja": sib}, device_id_type=MESH,
        )

    def sib_copy(chunk, source_z, slot, source_c):
        block = block_of(chunk, source_z, source_c)
        return pltpu.make_async_remote_copy(
            block, block, sib_send.at[chunk, slot], sib_recv.at[chunk, slot],
            device_id={"ja": sib}, device_id_type=MESH,
        )

    def last_hop(up, chunk):
        return 4 if up == (chunk < 2) else 3

    order = [(up, chunk) for pair in zip((0, 1, 2, 3), (2, 3, 0, 1)) for up, chunk in zip((True, False), pair)]
    for up, chunk in order:
        ring_copy(up, chunk, 1).start()

    def pass_on(hop):
        for up, chunk in order:
            if hop > last_hop(up, chunk):
                continue
            arrival(up, chunk, hop).wait_recv()
            if hop < last_hop(up, chunk):
                ring_copy(up, chunk, hop + 1).start()
            source = (z - hop + n_z) % n_z if up else (z + hop) % n_z
            sib_copy(chunk, source, hop if up else n_z - hop, c).start()

    def f2_copy(d):
        to = (ja + d) % n_ja
        return pltpu.make_async_remote_copy(
            f2_out.at[to], f2_in.at[ja], f2_send.at[to], f2_recv.at[ja],
            device_id={"ja": to}, device_id_type=MESH,
        )

    def f2_arrival(d):
        source = (ja + d) % n_ja
        return pltpu.make_async_remote_copy(
            f2_out.at[source], f2_in.at[source], f2_send.at[source], f2_recv.at[source],
            device_id={"ja": source}, device_id_type=MESH,
        )

    def start_f2(d, carry):
        f2_copy(d).start()
        return carry

    def start_half(h, carry):
        half_copy((x * 2 + 4 + h) % 8).start()
        return carry

    lax.fori_loop(0, 8, start_half, 0)
    lax.fori_loop(1, n_ja, start_f2, 0)
    for chunk in range(4):
        sib_copy(chunk, z, 0, c).start()
    def half_of(left, half):
        return slice(left + half * 256, left + (half + 1) * 256)

    def slab(axis, at, lanes):
        return (pl.ds(at, 1), slice(None), slice(None), lanes) if axis == 0 else (slice(None), pl.ds(at, 1), slice(None), lanes)

    def plane_copy(axis, way, kind):
        place = x if axis == 0 else y
        to = (place + (1, 3)[way]) % 4
        peer = (x_next, y_next)[axis][way]
        at = (place + 2) % 4 if kind == 0 else to
        half = 1 - way if kind == 1 else way
        lanes = half_of(axis * 512, half)
        source = to_plane.at[at, :, :, lanes] if axis == 0 else to_plane.at[:, at, :, lanes]
        target = far.at[axis, way] if kind == 0 else near.at[axis, way, :, :, half_of(0, half)]
        return pltpu.make_async_remote_copy(
            source, target, plane_send.at[axis, way, kind], plane_recv.at[axis, way, kind],
            device_id={"ka": peer}, device_id_type=MESH,
        )

    def cross_copy(axis, way, kind):
        place = y if axis == 0 else x
        to = (place + (1, 3)[way]) % 4
        peer = (y_next, x_next)[axis][way]
        at = (place + 2) % 4 if kind == 0 else to
        half = 1 - way if kind == 1 else way
        target = far_cross.at[axis, way] if kind == 0 else near_cross.at[axis, way, :, half_of(0, half)]
        return pltpu.make_async_remote_copy(
            to_cross.at[axis, at, :, half_of(0, half)], target,
            cross_send.at[axis, way, kind], cross_recv.at[axis, way, kind],
            device_id={"ka": peer}, device_id_type=MESH,
        )

    def combine(row):
        def body(h, carry):
            m = row * 2 + h
            half_copy(m).wait_recv()
            low, high = rows_of(m)
            to_plane[row, h * 2] = (low + from_sib[m, 0].astype(F32)).astype(BF16)
            to_plane[row, h * 2 + 1] = (high + from_sib[m, 1].astype(F32)).astype(BF16)
            return carry

        lax.fori_loop(0, 2, body, 0)

    combine((x + 2) % 4)
    for way in range(2):
        plane_copy(0, way, 0).start()
    combine((x + 1) % 4)
    plane_copy(0, 0, 1).start()
    combine((x + 3) % 4)
    plane_copy(0, 1, 1).start()
    combine(x)
    for kind in range(2):
        for way in range(2):
            plane_copy(1, way, kind).start()
    pass_on(1)

    for axis in range(2):
        place = x if axis == 0 else y
        for way in range(2):
            plane_copy(axis, way, 0).wait_recv()
            where = slab(axis, (place + (1, 3)[way]) % 4, half_of(axis * 512, way))
            mine = to_plane[where]
            to_plane[where] = (mine.astype(F32) + far[axis, way].reshape(mine.shape).astype(F32)).astype(BF16)
            plane_copy(axis, way, 2).start()
    pass_on(2)
    for axis in range(2):
        for way in range(2):
            for kind in (1, 2):
                plane_copy(axis, way, kind).wait_recv()
        mine = to_plane[slab(axis, x if axis == 0 else y, slice(axis * 512, axis * 512 + 512))].reshape(4, 32, 512)
        to_cross[axis] = (mine.astype(F32) + near[axis, 0].astype(F32) + near[axis, 1].astype(F32)).astype(BF16)
        for kind in range(2):
            for way in range(2):
                cross_copy(axis, way, kind).start()
    pass_on(3)
    pass_on(4)

    for axis in range(2):
        place = y if axis == 0 else x
        for way in range(2):
            cross_copy(axis, way, 0).wait_recv()
            where = (axis, (place + (1, 3)[way]) % 4, slice(None), half_of(0, way))
            to_cross[where] = (to_cross[where].astype(F32) + far_cross[axis, way].astype(F32)).astype(BF16)
            cross_copy(axis, way, 2).start()

    for slot in range(8):
        for chunk in range(4):
            sib_copy(chunk, (z - slot + n_z) % n_z, slot, 1 - c).wait_recv()

    own = core[:, pl.ds(own_row, 64), :]
    sums = []
    for block in range(4):
        columns = slice(block * 256, (block + 1) * 256)
        total = jnp.zeros((64, 256), F32)
        for k in range(4):
            total += lax.dot_general(
                own[k], core[k, columns, :], (((1,), (1,)), ((), ())), preferred_element_type=F32
            )
        sums.append(total)
    low, high = groups_of_four(sums)
    g2_out[:, 0] = low.astype(BF16)
    g2_out[:, 1] = high.astype(BF16)

    def g2_copy(to):
        return pltpu.make_async_remote_copy(
            g2_out.at[to // 2, to % 2], g2_in.at[ka], g2_send.at[to], g2_recv.at[ka],
            device_id={"ka": to}, device_id_type=MESH,
        )

    def g2_arrival(source):
        return pltpu.make_async_remote_copy(
            g2_out.at[source // 2, source % 2], g2_in.at[source], g2_send.at[source], g2_recv.at[source],
            device_id={"ka": source}, device_id_type=MESH,
        )

    def start_g2(d, carry):
        g2_copy((ka + d) % n_ka).start()
        return carry

    lax.fori_loop(1, n_ka, start_g2, 0)

    sides = []
    for axis in range(2):
        for way in range(2):
            for kind in (1, 2):
                cross_copy(axis, way, kind).wait_recv()
        mine = to_cross[axis, y if axis == 0 else x]
        sides.append(mine.astype(F32) + near_cross[axis, 0].astype(F32) + near_cross[axis, 1].astype(F32))
    total = jnp.concatenate(sides, axis=1)
    low, high = groups_of_four([total[:, i * 256 : (i + 1) * 256] for i in range(4)])
    to_line[:, 0] = low.astype(BF16)
    to_line[:, 1] = high.astype(BF16)

    def line_copy(to):
        return pltpu.make_async_remote_copy(
            to_line.at[to // 2, to % 2], from_line.at[z], line_send.at[to], line_recv.at[z],
            device_id={"ja": to * 2 + c}, device_id_type=MESH,
        )

    def line_arrival(source):
        return pltpu.make_async_remote_copy(
            to_line.at[source // 2, source % 2], from_line.at[source], line_send.at[source],
            line_recv.at[source], device_id={"ja": source * 2 + c}, device_id_type=MESH,
        )

    def start_line(d, carry):
        line_copy((z + d) % n_z).start()
        return carry

    lax.fori_loop(1, n_z, start_line, 0)

    def end_f2(d, carry):
        f2_arrival(d).wait_recv()
        return carry

    lax.fori_loop(1, n_ja, end_f2, 0)
    f2 = jnp.concatenate([f2_in[i].astype(F32) for i in range(n_ja)], axis=1).astype(BF16)
    for k in range(4):
        reduced[k] = jnp.dot(f2, core[k], preferred_element_type=F32)

    def add_g2(d, total):
        source = (ka + d) % n_ka
        g2_arrival(source).wait_recv()
        return total + g2_in[source].astype(F32)

    total = lax.fori_loop(1, n_ka, add_g2, g2_out[ka // 2, ka % 2].astype(F32)) * norms[1]
    for i in range(4):
        gram_two[:, i * 256 : (i + 1) * 256] = total[i * 4 : (i + 1) * 4]

    def add_line(d, total):
        source = (z + d) % n_z
        line_arrival(source).wait_recv()
        return total + from_line[source].astype(F32)

    total = lax.fori_loop(1, n_z, add_line, to_line[z // 2, z % 2].astype(F32)) * norms[0]
    for i in range(4):
        gram_one[:, i * 256 : (i + 1) * 256] = total[i * 4 : (i + 1) * 4]

    for chunk in range(4):
        for up in (True, False):
            for hop in range(1, last_hop(up, chunk) + 1):
                ring_copy(up, chunk, hop).wait_send()
        for slot in range(8):
            sib_copy(chunk, (z - slot + n_z) % n_z, slot, c).wait_send()
    for axis in range(2):
        for way in range(2):
            for kind in range(3):
                plane_copy(axis, way, kind).wait_send()
                cross_copy(axis, way, kind).wait_send()

    def end_ja(d, carry):
        f2_copy(d).wait_send()
        return carry

    def end_ka(d, carry):
        g2_copy((ka + d) % n_ka).wait_send()
        return carry

    def end_z(d, carry):
        line_copy((z + d) % n_z).wait_send()
        return carry

    def end_half(m, carry):
        half_copy(m).wait_send()
        return carry

    lax.fori_loop(1, n_ja, end_ja, 0)
    lax.fori_loop(1, n_ka, end_ka, 0)
    lax.fori_loop(1, n_z, end_z, 0)
    lax.fori_loop(0, 8, end_half, 0)


def solution(mesh):
    n_ja, n_ka = mesh.shape["ja"], mesh.shape["ka"]

    def shards(tensor, factor_one, factor_two):
        slices, owned, width = tensor.shape
        norm_one = 1.0 / math.sqrt(owned * n_ja * slices * n_ka)
        norm_two = 1.0 / math.sqrt(slices * n_ka * factor_one.shape[1])
        dma = pltpu.SemaphoreType.DMA

        def body(*refs):
            kernel((norm_one, norm_two), (n_ja, n_ka), *refs)

        return pl.pallas_call(
            body,
            out_shape=(
                jax.ShapeDtypeStruct((4, 1024), F32),
                jax.ShapeDtypeStruct((4, 1024), F32),
                jax.ShapeDtypeStruct((4, 16, 256), F32),
            ),
            in_specs=[pl.BlockSpec(memory_space=pl.ANY)] * 3,
            out_specs=[pl.BlockSpec(memory_space=pltpu.VMEM)] * 3,
            scratch_shapes=[
                pltpu.VMEM((4, 64, 1024), F32),
                pltpu.VMEM((1024, 256), F32),
                pltpu.VMEM((64, 256), BF16),
                pltpu.VMEM((2, 8, 64, 768), BF16),
                pltpu.VMEM((768, 1024), BF16),
                pltpu.VMEM((8, 64, 1024), F32),
                pltpu.VMEM((8, 2, 32, 1024), BF16),
                pltpu.VMEM((8, 2, 32, 1024), BF16),
                pltpu.VMEM((4, 4, 32, 1024), BF16),
                pltpu.VMEM((2, 2, 4, 32, 256), BF16),
                pltpu.VMEM((2, 2, 4, 32, 512), BF16),
                pltpu.VMEM((2, 4, 32, 512), BF16),
                pltpu.VMEM((2, 2, 32, 256), BF16),
                pltpu.VMEM((2, 2, 32, 512), BF16),
                pltpu.VMEM((4, 2, 16, 256), BF16),
                pltpu.VMEM((8, 16, 256), BF16),
                pltpu.VMEM((4, 1024, 256), BF16),
                pltpu.VMEM((16, 16, 64), BF16),
                pltpu.VMEM((16, 16, 64), BF16),
                pltpu.VMEM((8, 2, 16, 256), BF16),
                pltpu.VMEM((16, 16, 256), BF16),
                dma((3,)),
                dma((4, 4)), dma((4, 4)), dma((4, 4)), dma((4, 4)),
                dma((4, 8)), dma((4, 8)),
                dma((8,)), dma((8,)),
                dma((2, 2, 3)), dma((2, 2, 3)),
                dma((2, 2, 3)), dma((2, 2, 3)),
                dma((8,)), dma((8,)),
                dma((16,)), dma((16,)),
                dma((16,)), dma((16,)),
            ],
            compiler_params=pltpu.CompilerParams(
                collective_id=0, has_side_effects=True, vmem_limit_bytes=48 * 1024 * 1024
            ),
        )(tensor, factor_one, factor_two)

    return jax.shard_map(
        shards,
        mesh=mesh,
        in_specs=(P("ka", "ja", None), P(), P("ja", None)),
        out_specs=(P(("ja", "ka"), None), P(("ja", "ka"), None), P("ka", "ja", None)),
        check_vma=False,
    )
```
